1024 devices in a mesh: group: 32 (over y, x, core), shuf: 32 (over z).
Axes of the slice: x: 4, y: 4, z: 32, core: 2. Of those that a mesh axis runs over, the one named last changes fastest.
Arguments:
- inputs: bfloat16 [32, 8192, 512], P('group', 'shuf'), may hold values from -8 to 8
- cotangent: bfloat16 [32, 8192, 512], P('group', 'shuf'), may hold values from -8 to 8
- w_uvqk: bfloat16 [512, 2048], P('group'), may hold values from -0.25 to 0.25
- w_out: bfloat16 [512, 512], P('group'), may hold values from -0.25 to 0.25
- send_perm: int32 [32, 32, 32], P('group', 'shuf'), may hold values from 0 to 31, each once within a row
- recv_perm: int32 [32, 32, 32], P('group', 'shuf'), may hold values from 0 to 31, each once within a row
- lengths: int32 [32, 32, 8], P('group', 'shuf'), may hold values from 1 to 128, 256 in all within a row
- prefixes: int32 [32, 32, 8], P('group', 'shuf'), may hold values from 0 to 32
Outputs:
- layer_out: bfloat16 [32, 8192, 512], P('group', 'shuf')
- grad_input: bfloat16 [32, 8192, 512], P('group', 'shuf')
- grad_uvqk: float32 [512, 2048], P('group')
- grad_wout: float32 [512, 512], P('group')
The draws below stay inside these ranges and needn't reach their ends.
All inputs are finite; a program needn't handle non-finite values.
Results may differ from the reference program's by a relative error of at most 0.03.
Values may be sent and summed in bfloat16 or wider, within the bound.
A program may use at most 32 MiB of HBM per device.

```python
import math
from functools import partial
import jax
import jax.numpy as jnp
import numpy as np
from jax import lax

D = 512
HEADS = 8
ROWS = 256
BLOCK = 8
USERS = 8
BLK_DEV = 32
CAP = 1
MAX_LEN = 128
N_GROUP = 32
N_SHUF = 32


def set_ends(array, rng, least, top_value):
    longest = array.shape.index(max(array.shape))
    spots = []
    for shift in (0, 1):
        where = [jax.random.randint(jax.random.fold_in(rng, axis), (), 0, length) for axis, length in enumerate(array.shape)]
        where[longest] = (where[longest] + shift) % array.shape[longest]
        spots.append(tuple(where))
    return array.at[spots[0]].set(least).at[spots[1]].set(top_value)


def with_spikes(values, key, source, target, parts, factor):
    def block_of(axis_at):
        return (jnp.arange(values.shape[axis_at]) // (values.shape[axis_at] // parts)).reshape((-1,) + (1,) * (values.ndim - 1 - axis_at))

    first = jax.random.permutation(key, parts)[block_of(target)]
    other_side = (block_of(target) + parts // 2) % parts
    return jnp.where((block_of(source) == first) | (block_of(source) == other_side), factor * values, values)


def steps_of(key, dims, shards, smallest, largest):
    def one(dim, shards_of):
        heights = jax.random.uniform(jax.random.fold_in(jax.random.fold_in(key, 6), dim), (shards_of,), jnp.float32, smallest / len(shards), largest / len(shards))
        return jnp.repeat(jnp.exp(heights), dims[dim] // shards_of).reshape((-1,) + (1,) * (len(dims) - dim - 1))

    gain = one(*shards[0])
    for cut in shards[1:]:
        gain = gain * one(*cut)
    return gain


def split_up(number_of, total, limit, lean):
    portions = [(1 << 20) // math.isqrt(rank ** lean) + 1 for rank in range(2, number_of + 1)]
    surplus, holding = total - limit - (number_of - 1), [1] * (number_of - 1)
    while surplus > 0:
        movable = [i for i in range(number_of - 1) if holding[i] < limit]
        whole, remaining = sum([portions[i] for i in movable]), surplus
        for i in movable:
            more = min(limit - holding[i], max(1, remaining * portions[i] // whole), surplus)
            holding[i] = holding[i] + more
            surplus = surplus - more
    return np.array([limit] + holding)


def ragged_sizes(own_key, count, total, bound, lean):
    if count == 2:
        one = jax.random.randint(own_key, (), max(1, total - bound), min(bound, total - 1) + 1)
        return jnp.stack([one, total - one])
    sizes = jnp.asarray(split_up(count, total, bound, lean), jnp.int32)
    pairs = (count - 1) // 2
    giver, receiver = sizes[1:1 + 2 * pairs:2], sizes[2:2 + 2 * pairs:2]
    slack = jnp.minimum(giver - 1, bound - receiver)
    shifted = jax.random.randint(jax.random.fold_in(own_key, 1), (pairs,), 0, 1 << 20) % (slack + 1)
    sizes = sizes.at[1:1 + 2 * pairs:2].set(giver - shifted).at[2:2 + 2 * pairs:2].set(receiver + shifted)
    return sizes[jax.random.permutation(jax.random.fold_in(own_key, 2), count)]


def noise(stream_key, shape, spread, bound, split=(), kind=jnp.bfloat16):
    result = spread * jax.random.normal(stream_key, shape, jnp.float32)
    if split:
        result = result * steps_of(stream_key, shape, split, -0.22, 0.18)
    return jnp.clip(result, -bound, bound).astype(kind)


def gaussian_with(own_key, extent, scale, limit, cuts, heavy, kind=jnp.bfloat16):
    values = scale * jax.random.normal(own_key, extent, jnp.float32)
    if cuts:
        values = values * steps_of(own_key, extent, cuts, -0.22, 0.18)
    return jnp.clip(with_spikes(values, jax.random.fold_in(own_key, 3), *heavy), -limit, limit).astype(kind)


def setup_inputs(seed: int = 0) -> dict:
    arg_keys = jax.random.split(jax.random.key(seed), 9)
    inputs = gaussian_with(arg_keys[0], (N_GROUP, N_SHUF * ROWS, D), 1.0, 8.0, ((0, 32), (1, 32)), (0, 2, 32, 2.75))
    cotangent = noise(arg_keys[1], (N_GROUP, N_SHUF * ROWS, D), 1.0, 8.0, ((0, 32), (1, 32)))
    w_uvqk = noise(arg_keys[2], (D, 4 * D), D ** -0.5, 0.25, ((0, 32),))
    w_out = noise(arg_keys[3], (D, D), D ** -0.5, 0.25, ((0, 32),))
    send_perm = jax.vmap(lambda own: jax.random.permutation(own, BLK_DEV))(jax.random.split(arg_keys[4], N_GROUP * N_SHUF)).reshape((N_GROUP, N_SHUF, BLK_DEV)).astype(jnp.int32)
    recv_perm = jax.vmap(lambda own: jax.random.permutation(own, BLK_DEV))(jax.random.split(arg_keys[5], N_GROUP * N_SHUF)).reshape((N_GROUP, N_SHUF, BLK_DEV)).astype(jnp.int32)
    lengths = jax.vmap(lambda own: ragged_sizes(own, USERS, ROWS, MAX_LEN, 2))(jax.random.split(arg_keys[6], N_GROUP * N_SHUF)).reshape((N_GROUP, N_SHUF, USERS)).astype(jnp.int32)
    prefixes = set_ends(jax.random.randint(arg_keys[7], (N_GROUP, N_SHUF, USERS), 0, MAX_LEN // 4 + 1), jax.random.fold_in(arg_keys[7], 1), 0, (MAX_LEN // 4 + 1) - 1).astype(jnp.int32)
    return dict(inputs=inputs, cotangent=cotangent, w_uvqk=w_uvqk, w_out=w_out, send_perm=send_perm, recv_perm=recv_perm, lengths=lengths, prefixes=prefixes)


norm_eps = 1e-05

def normalize(values):
    center = lax.optimization_barrier(jnp.mean(values, axis=-1, keepdims=True))
    centred = values - center
    variance = lax.optimization_barrier(jnp.mean(centred * centred, axis=-1, keepdims=True))
    inv_scale = lax.rsqrt(variance + norm_eps)
    return (centred * inv_scale, inv_scale)

def silu_slope(values):
    sigma = jax.nn.sigmoid(values)
    return sigma * (1.0 + values * (1.0 - sigma))

def visible(user_lengths, user_prefixes, row_count):
    user_ends = jnp.cumsum(user_lengths).astype(jnp.int32)
    row_index = jnp.arange(row_count, dtype=jnp.int32)
    user_index = lax.optimization_barrier(jnp.sum((row_index[:, None] >= user_ends[None, :]).astype(jnp.int32), axis=1)).astype(jnp.int32)
    member = user_index[:, None] == jnp.arange(user_lengths.shape[0], dtype=jnp.int32)[None, :]
    starts = (user_ends - user_lengths).astype(jnp.int32)
    position = row_index - lax.optimization_barrier(jnp.sum(jnp.where(member, starts[None, :], 0), axis=1)).astype(jnp.int32)
    prefix_len = lax.optimization_barrier(jnp.sum(jnp.where(member, user_prefixes[None, :], 0), axis=1)).astype(jnp.int32)
    same_user = user_index[:, None] == user_index[None, :]
    return same_user & ((row_index[None, :] <= row_index[:, None]) | (position[None, :] < prefix_len[:, None]))

def attention(activated, weight_out, residual, allowed):
    row_count = activated.shape[0]
    gate_u = activated[:, :D]
    values = activated[:, D:2 * D].reshape(row_count, HEADS, D // HEADS)
    queries = activated[:, 2 * D:3 * D].reshape(row_count, HEADS, D // HEADS)
    keys = activated[:, 3 * D:].reshape(row_count, HEADS, D // HEADS)
    scores = jnp.einsum('qhd,khd->hqk', queries.astype(jnp.float32), keys.astype(jnp.float32))
    weights = (jnp.where(allowed[None], jax.nn.silu(scores), 0.0) / ROWS).astype(jnp.bfloat16)
    mixed = jnp.einsum('hqk,khd->qhd', weights.astype(jnp.float32), values.astype(jnp.float32)).reshape(row_count, D)
    normed, unused = normalize(mixed)
    gated = (normed * gate_u.astype(jnp.float32)).astype(jnp.bfloat16)
    return (jnp.dot(gated, weight_out, preferred_element_type=jnp.float32) + residual).astype(jnp.bfloat16)

def device_pass(rows_x, rows_cot, w_uvqk, w_out, user_lengths, user_prefixes):
    inputs_f32 = rows_x.astype(jnp.float32)
    centred, inv_scale = normalize(inputs_f32)
    normed_x = centred.astype(jnp.bfloat16)
    projected = jnp.dot(normed_x, w_uvqk, preferred_element_type=jnp.float32)
    activated = jax.nn.silu(projected).astype(jnp.bfloat16)
    allowed = visible(user_lengths, user_prefixes, rows_x.shape[0])
    layer_value, pullback = jax.vjp(partial(attention, allowed=allowed), activated, w_out, inputs_f32)
    grad_act, grad_weight, grad_res = pullback(rows_cot)
    grad_proj = (grad_act.astype(jnp.float32) * silu_slope(projected)).astype(jnp.bfloat16)
    part_uvqk = lax.dot_general(normed_x, grad_proj, (((0,), (0,)), ((), ())), preferred_element_type=jnp.float32)
    grad_normed = lax.dot_general(grad_proj, w_uvqk, (((1,), (1,)), ((), ())), preferred_element_type=jnp.float32)
    grad_center = lax.optimization_barrier(jnp.mean(grad_normed, axis=-1, keepdims=True))
    grad_proj_z = lax.optimization_barrier(jnp.mean(grad_normed * centred, axis=-1, keepdims=True))
    grad_rows = inv_scale * (grad_normed - grad_center - centred * grad_proj_z) + grad_res.astype(jnp.float32)
    return (layer_value, grad_rows.astype(jnp.bfloat16), part_uvqk, grad_weight.astype(jnp.float32))

def reference(inputs, cotangent, w_uvqk, w_out, send_perm, recv_perm, lengths, prefixes):
    groups = N_GROUP
    peers = N_SHUF
    blocks = BLK_DEV
    input_blocks = inputs.reshape(groups, peers * blocks, BLOCK, D)
    cot_blocks = cotangent.reshape(groups, peers * blocks, BLOCK, D)
    source_dev = (recv_perm // CAP).astype(jnp.int32)
    sub_slot = (recv_perm % CAP).astype(jnp.int32)
    target = jnp.arange(peers, dtype=jnp.int32)[None, :, None]
    send_pos = (target * CAP + sub_slot).astype(jnp.int32)
    group_index = jnp.arange(groups, dtype=jnp.int32)[:, None, None]
    block_id = send_perm[group_index, source_dev, send_pos]
    src_flat = (source_dev * blocks + block_id).reshape(groups, peers * blocks).astype(jnp.int32)
    bal_x = jnp.take_along_axis(input_blocks, src_flat[:, :, None, None], axis=1).reshape(groups * peers, ROWS, D)
    bal_cot = jnp.take_along_axis(cot_blocks, src_flat[:, :, None, None], axis=1).reshape(groups * peers, ROWS, D)
    user_lens = lengths.reshape(groups * peers, USERS)
    user_pref = prefixes.reshape(groups * peers, USERS)

    def step(totals, device_items):
        layer_value, grad_rows, part_uvqk, part_wout = device_pass(device_items[0], device_items[1], w_uvqk, w_out, device_items[2], device_items[3])
        rounded = lax.optimization_barrier(part_uvqk.astype(jnp.bfloat16)).astype(jnp.float32)
        return ((totals[0] + rounded, totals[1] + part_wout), (layer_value, grad_rows))
    start_totals = (jnp.zeros((D, 4 * D), jnp.float32), jnp.zeros((D, D), jnp.float32))
    totals, outputs = lax.scan(step, start_totals, (bal_x, bal_cot, user_lens, user_pref))
    inverse_map = jnp.zeros((groups, peers * blocks), jnp.int32).at[jnp.arange(groups, dtype=jnp.int32)[:, None], src_flat].set(jnp.broadcast_to(jnp.arange(peers * blocks, dtype=jnp.int32)[None, :], (groups, peers * blocks)))
    out_blocks = outputs[0].reshape(groups, peers * blocks, BLOCK, D)
    grad_blocks = outputs[1].reshape(groups, peers * blocks, BLOCK, D)
    layer_out = jnp.take_along_axis(out_blocks, inverse_map[:, :, None, None], axis=1).reshape(groups, peers * ROWS, D)
    grad_input = jnp.take_along_axis(grad_blocks, inverse_map[:, :, None, None], axis=1).reshape(groups, peers * ROWS, D)
    return (layer_out, grad_input, totals[0], totals[1])
```

```python
import jax
import jax.numpy as jnp
from jax import lax
from jax.experimental import pallas as pl
from jax.experimental.pallas import tpu as pltpu
from jax.sharding import PartitionSpec as P

D = 512
HEADS = 8
ROWS = 256
BLOCK = 8
BLK = 32
USERS = 8
NZ = 32
SEG = 8
NSEG = 4
COLS = 2560
HALF = 1280
QUART = 640
EPS = 1e-05
MESH = pl.DeviceIdType.MESH
F32 = jnp.float32
BF16 = jnp.bfloat16


def dot(a, b, ca, cb):
    return lax.dot_general(a, b, (((ca,), (cb,)), ((), ())), preferred_element_type=F32)


def kernel(
    x_in, c_in, wu_in, wo_in, sp_in, rp_in, len_in, pre_in,
    out_ref, grad_ref, gu_ref, go_ref,
    xs, xr, cs, cr, os_, or_, gs, gr,
    wfull, pb, rc, sa, sb, sa2, sb2, ta, tb, ta2, tb2, ua, ub, ua2, ub2,
    z1, r1, z2, r2, z3, r3,
    pts, ptr, vis, xf, zf, inv, xn, act, dact, mixed, gated, gproj, w8, d8,
    a2a_send, a2a_recv, ag_send, ag_recv, rs_send, rs_recv, ar_send, ar_recv,
):
    g = lax.axis_index("group")
    z = lax.axis_index("shuf")
    core = g % 2
    xx = (g // 2) % 4
    yy = g // 8

    def gid(y, x, c):
        return (y * 4 + x) * 2 + c

    xplus = (gid(yy, (xx + 1) % 4, core), z)
    xminus = (gid(yy, (xx + 3) % 4, core), z)
    yplus = (gid((yy + 1) % 4, xx, core), z)
    yminus = (gid((yy + 3) % 4, xx, core), z)
    partner = (gid(yy, xx, 1 - core), z)

    def remote(src, dst, ssem, rsem, dev):
        return pltpu.make_async_remote_copy(
            src_ref=src, dst_ref=dst, send_sem=ssem, recv_sem=rsem,
            device_id=dev, device_id_type=MESH,
        )

    barrier = pltpu.get_barrier_semaphore()
    for dev in (xplus, xminus, yplus, yminus, partner):
        pl.semaphore_signal(barrier, inc=1, device_id=dev, device_id_type=MESH)

    def greet(k, carry):
        pl.semaphore_signal(
            barrier, inc=1, device_id=(g, (z + 1 + k) % NZ), device_id_type=MESH
        )
        return carry

    lax.fori_loop(0, NZ - 1, greet, 0)

    lane = lax.broadcasted_iota(jnp.int32, (1, ROWS), 1)
    row_of = lax.broadcasted_iota(jnp.int32, (ROWS, ROWS), 0)

    def one_hot(perm_ref):
        index = lane % BLOCK
        for t in range(BLK):
            index = index + jnp.where(lane // BLOCK == t, perm_ref[t] * BLOCK, 0)
        return (row_of == index).astype(F32).astype(BF16)

    pts[...] = one_hot(sp_in)
    ptr[...] = one_hot(rp_in)

    def to_blocks(value):
        return value.reshape(BLK, BLOCK, D).astype(BF16)

    def rows_of(ref):
        return ref[...].astype(F32).reshape(ROWS, D)

    xs[...] = to_blocks(dot(pts[...], x_in[...], 0, 0))
    cs[...] = to_blocks(dot(pts[...], c_in[...], 0, 0))
    xr[z] = xs[z]
    cr[z] = cs[z]

    wfull[yy, xx, core, :, 0 : 4 * D] = wu_in[...]
    wfull[yy, xx, core, :, 4 * D : COLS] = wo_in[...]
    ri = lax.broadcasted_iota(jnp.int32, (ROWS, 1), 0)
    uid_r = jnp.zeros((ROWS, 1), jnp.int32)
    uid_k = jnp.zeros((1, ROWS), jnp.int32)
    pre_r = jnp.zeros((ROWS, 1), jnp.int32) + pre_in[0]
    start_k = jnp.zeros((1, ROWS), jnp.int32)
    end = len_in[0]
    for u in range(USERS):
        past_r = ri >= end
        past_k = lane >= end
        uid_r = uid_r + jnp.where(past_r, 1, 0)
        uid_k = uid_k + jnp.where(past_k, 1, 0)
        start_k = start_k + jnp.where(past_k, len_in[u], 0)
        if u < USERS - 1:
            pre_r = pre_r + jnp.where(past_r, pre_in[u + 1] - pre_in[u], 0)
            end = end + len_in[u + 1]
    allowed = jnp.where(
        uid_r == uid_k,
        jnp.where(lane <= ri, 1.0, jnp.where(lane - start_k < pre_r, 1.0, 0.0)),
        0.0,
    )
    vis[...] = allowed * (1.0 / ROWS)

    pl.semaphore_wait(barrier, NZ - 1 + 5)

    def exchange(which, src, dst, first, last, near):
        def step(k, carry):
            j = NZ - 2 - k if near else k
            m = (j + 1) // 2
            off = NZ // 2 + m * (2 * (j % 2) - 1)
            peer = (z + off) % NZ
            remote(
                src.at[peer], dst.at[z], a2a_send.at[which], a2a_recv.at[which], (g, peer)
            ).start()
            return carry

        lax.fori_loop(first, last, step, 0)

    def exchange_wait(which, buf, recv):
        part = buf.at[pl.ds(0, NZ - 1)]
        copy = remote(
            part, part, a2a_send.at[which], a2a_recv.at[which], (g, (z + 1) % NZ)
        )
        if recv:
            copy.wait_recv()
        else:
            copy.wait_send()

    exchange(0, xs, xr, 0, NZ - 1, True)

    own = wfull.at[yy, xx, core]
    w_x0 = remote(own, own, ag_send.at[0], ag_recv.at[0], xplus)
    w_x1 = remote(own, own, ag_send.at[1], ag_recv.at[1], xminus)
    w_x0.start()
    w_x1.start()
    exchange(1, cs, cr, 0, NZ - 1, False)

    def half_x(x, h):
        return wfull.at[yy, x, core, :, pl.ds(h * HALF, HALF)]

    w_x0.wait_recv()
    left = half_x((xx + 3) % 4, 0)
    w_x2 = remote(left, left, ag_send.at[2], ag_recv.at[2], xplus)
    w_x2.start()
    w_x1.wait_recv()
    right = half_x((xx + 1) % 4, 1)
    w_x3 = remote(right, right, ag_send.at[3], ag_recv.at[3], xminus)
    w_x3.start()
    w_x2.wait_recv()
    w_x3.wait_recv()
    mine = wfull.at[yy, :, core]
    w_y0 = remote(mine, mine, ag_send.at[4], ag_recv.at[4], yplus)
    w_y1 = remote(mine, mine, ag_send.at[5], ag_recv.at[5], yminus)
    w_y0.start()
    w_y1.start()

    def half_y(y, h):
        return wfull.at[y, pl.ds(2 * h, 2), core]

    w_y0.wait_recv()
    down = half_y((yy + 3) % 4, 0)
    w_y2 = remote(down, down, ag_send.at[6], ag_recv.at[6], yplus)
    w_y2.start()
    w_y1.wait_recv()
    up = half_y((yy + 1) % 4, 1)
    w_y3 = remote(up, up, ag_send.at[7], ag_recv.at[7], yminus)
    w_y3.start()
    w_y2.wait_recv()
    w_y3.wait_recv()
    column = wfull.at[:, :, core]
    w_c = remote(column, column, ag_send.at[8], ag_recv.at[8], partner)
    w_c.start()

    exchange_wait(0, xr, True)
    x32 = dot(ptr[...], rows_of(xr).astype(BF16), 0, 0)
    xf[...] = x32
    center = jnp.mean(x32, axis=-1, keepdims=True)
    centred = x32 - center
    scale = lax.rsqrt(jnp.mean(centred * centred, axis=-1, keepdims=True) + EPS)
    inv[...] = jnp.broadcast_to(scale, (ROWS, 128))
    normed_x = centred * scale
    zf[...] = normed_x
    xn[...] = normed_x.astype(BF16)
    w_c.wait_recv()

    def weight(c):
        return wfull[:, :, :, :, pl.ds(pl.multiple_of(c * D, D), D)].reshape(D, D)

    def project(c, carry):
        cols = pl.ds(pl.multiple_of(c * D, D), D)
        p = dot(xn[...], weight(c), 1, 0)
        s = jax.nn.sigmoid(p)
        act[:, cols] = (p * s).astype(BF16)
        dact[:, cols] = s * (1.0 + p * (1.0 - s))
        return carry

    lax.fori_loop(0, 4, project, 0)

    lane128 = lax.broadcasted_iota(jnp.int32, (ROWS, 128), 1)

    def pair_cols(base, p):
        return pl.ds(pl.multiple_of(base * D + p * 128, 128), 128)

    def attend(p, carry):
        v = act[:, pair_cols(1, p)]
        q = act[:, pair_cols(2, p)].astype(F32)
        k = act[:, pair_cols(3, p)]
        parts = []
        for h in range(2):
            inside = (lane128 // 64) == h
            qh = jnp.where(inside, q, 0.0).astype(BF16)
            scores = dot(qh, k, 1, 1)
            s = jax.nn.sigmoid(scores)
            allow = vis[...]
            wts = (scores * s * allow).astype(BF16)
            w8[2 * p + h] = wts
            d8[2 * p + h] = s * (1.0 + scores * (1.0 - s)) * allow
            parts.append(dot(wts, v, 1, 0))
        mixed[:, pl.ds(pl.multiple_of(p * 128, 128), 128)] = jnp.where(
            lane128 < 64, parts[0], parts[1]
        )
        return carry

    lax.fori_loop(0, HEADS // 2, attend, 0)

    m32 = mixed[...]
    m_center = jnp.mean(m32, axis=-1, keepdims=True)
    m_centred = m32 - m_center
    m_scale = lax.rsqrt(jnp.mean(m_centred * m_centred, axis=-1, keepdims=True) + EPS)
    m_normed = m_centred * m_scale
    mixed[...] = m_normed
    gated[...] = (m_normed * act[:, 0:D].astype(F32)).astype(BF16)
    layer = (dot(gated[...], weight(4), 1, 0) + xf[...]).astype(BF16)
    os_[...] = to_blocks(dot(ptr[...], layer, 1, 0))
    or_[z] = os_[z]
    exchange(2, os_, or_, 0, NZ - 1, False)

    exchange_wait(1, cr, True)
    cot = dot(ptr[...], rows_of(cr).astype(BF16), 0, 0)
    cot16 = cot.astype(BF16)
    xf[...] = cot
    pb[:, :, :, :, 4 * D : COLS] = (
        dot(gated[...], cot16, 0, 0).astype(BF16).reshape(4, 4, 2, 16, D)
    )
    g_gated = dot(cot16, weight(4), 1, 1).astype(BF16).astype(F32)
    m_normed = mixed[...]
    g_normed = g_gated * act[:, 0:D].astype(F32)
    g_u = (g_gated * m_normed).astype(BF16).astype(F32)
    gproj[:, 0:D] = (g_u * dact[:, 0:D]).astype(BF16)
    g_mixed = m_scale * (
        g_normed
        - jnp.mean(g_normed, axis=-1, keepdims=True)
        - m_normed * jnp.mean(g_normed * m_normed, axis=-1, keepdims=True)
    )
    gated[...] = g_mixed.astype(BF16)

    def attend_back(p, carry):
        v = act[:, pair_cols(1, p)]
        q = act[:, pair_cols(2, p)]
        k = act[:, pair_cols(3, p)]
        gm = gated[:, pl.ds(pl.multiple_of(p * 128, 128), 128)]
        gv, gq, gk = [], [], []
        for h in range(2):
            inside = (lane128 // 64) == h
            gmh = jnp.where(inside, gm.astype(F32), 0.0).astype(BF16)
            g_w = dot(gmh, v, 1, 1).astype(BF16).astype(F32)
            g_s = (g_w * d8[2 * p + h]).astype(BF16)
            gv.append(dot(w8[2 * p + h], gm, 0, 0))
            gq.append(dot(g_s, k, 1, 0))
            gk.append(dot(g_s, q, 0, 0))
        for base, part in ((1, gv), (2, gq), (3, gk)):
            value = jnp.where(lane128 < 64, part[0], part[1]).astype(BF16).astype(F32)
            cols = pair_cols(base, p)
            gproj[:, cols] = (value * dact[:, cols]).astype(BF16)
        return carry

    lax.fori_loop(0, HEADS // 2, attend_back, 0)

    def weight_grad(c, carry):
        cols = pl.ds(pl.multiple_of(c * D, D), D)
        part = dot(xn[...], gproj[:, cols], 0, 0)
        pb[:, :, :, :, cols] = part.astype(BF16).reshape(4, 4, 2, 16, D)
        return carry

    lax.fori_loop(0, 4, weight_grad, 0)

    other = pb.at[:, :, 1 - core]
    p_c = remote(other, rc, rs_send.at[0], rs_recv.at[0], partner)
    p_c.start()

    mixed[...] = dot(gproj[:, 0:D], weight(0), 1, 1)

    def input_grad(c, carry):
        cols = pl.ds(pl.multiple_of(c * D, D), D)
        mixed[...] = mixed[...] + dot(gproj[:, cols], weight(c), 1, 1)
        return carry

    lax.fori_loop(1, 4, input_grad, 0)
    g_xn = mixed[...]
    zz = zf[...]
    g_x = inv[:, 0:1] * (
        g_xn
        - jnp.mean(g_xn, axis=-1, keepdims=True)
        - zz * jnp.mean(g_xn * zz, axis=-1, keepdims=True)
    ) + xf[...]
    gs[...] = to_blocks(dot(ptr[...], g_x.astype(BF16), 1, 0))
    gr[z] = gs[z]
    exchange(3, gs, gr, 0, 8, False)

    p_c.wait_recv()

    def core_sum(i, carry):
        y = i // 4
        x = i % 4
        total = (pb[y, x, core].astype(F32) + rc[y, x].astype(F32)).astype(BF16)
        sa[y, x // 2, x % 2] = total[:, 0:HALF]
        sb[x, y // 2, y % 2] = total[:, HALF:COLS]
        return carry

    lax.fori_loop(0, 16, core_sum, 0)

    def ring_open(base, me, plus, minus, s, t, u):
        opp, nxt, prv = (me + 2) % 4, (me + 1) % 4, (me + 3) % 4
        plan = (
            (s.at[opp, 0], t.at[0], plus),
            (s.at[opp, 1], t.at[1], minus),
            (s.at[nxt, 1], u.at[0, 1], plus),
            (s.at[prv, 0], u.at[1, 0], minus),
            (s.at[nxt, 0], u.at[0, 0], plus),
            (s.at[prv, 1], u.at[1, 1], minus),
        )
        copies = [
            remote(src, dst, rs_send.at[base + i], rs_recv.at[base + i], dev)
            for i, (src, dst, dev) in enumerate(plan)
        ]
        for copy in copies[:4]:
            copy.start()
        return copies

    def ring_pass(copies, me, s, t):
        nxt, prv = (me + 1) % 4, (me + 3) % 4
        copies[0].wait_recv()
        s[nxt, 0] = (s[nxt, 0].astype(F32) + t[0].astype(F32)).astype(BF16)
        copies[4].start()
        copies[1].wait_recv()
        s[prv, 1] = (s[prv, 1].astype(F32) + t[1].astype(F32)).astype(BF16)
        copies[5].start()

    def ring_close(copies, me, s, u, h):
        return s[me, h].astype(F32) + u[0, h].astype(F32) + u[1, h].astype(F32)

    ca = ring_open(1, yy, yplus, yminus, sa, ta, ua)
    cb = ring_open(7, xx, xplus, xminus, sb, tb, ub)
    ring_pass(ca, yy, sa, ta)
    ring_pass(cb, xx, sb, tb)
    for copies in (ca, cb):
        for i in range(2, 6):
            copies[i].wait_recv()
    for h in range(2):
        total = ring_close(ca, yy, sa, ua, h).astype(BF16)
        for i in range(2):
            for q in range(2):
                sa2[2 * h + i, q] = total[i, :, q * QUART : (q + 1) * QUART]
    for h in range(2):
        total = ring_close(cb, xx, sb, ub, h).astype(BF16)
        for i in range(2):
            for q in range(2):
                sb2[2 * h + i, q] = total[i, :, q * QUART : (q + 1) * QUART]
    ca2 = ring_open(13, xx, xplus, xminus, sa2, ta2, ua2)
    cb2 = ring_open(19, yy, yplus, yminus, sb2, tb2, ub2)
    ring_pass(ca2, xx, sa2, ta2)
    ring_pass(cb2, yy, sb2, tb2)
    for copies in (ca2, cb2):
        for i in range(2, 6):
            copies[i].wait_recv()
    for which, (copies, me, s, u) in enumerate(((ca2, xx, sa2, ua2), (cb2, yy, sb2, ub2))):
        for h in range(2):
            total = ring_close(copies, me, s, u, h)
            for j in range(5):
                for r in range(2):
                    k = ((which * 2 + h) * 5 + j) * 2 + r
                    z1[k // 5, k % 5] = total[
                        8 * r : 8 * r + 8, 128 * j : 128 * j + 128
                    ].astype(BF16)

    seg = z // SEG
    idx = z % SEG

    def in_segment(d):
        i = (idx + d) % SEG
        return i, (g, seg * SEG + i)

    def scatter_step(d, carry):
        i, dev = in_segment(d)
        remote(z1.at[i], r1.at[idx], ar_send.at[0], ar_recv.at[0], dev).start()
        return carry

    lax.fori_loop(1, SEG, scatter_step, 0)
    exchange(3, gs, gr, 8, 16, False)
    r1[idx] = z1[idx]
    seven = r1.at[pl.ds(0, SEG - 1)]
    remote(seven, seven, ar_send.at[0], ar_recv.at[0], partner).wait_recv()
    total = r1[0].astype(F32)
    for i in range(1, SEG):
        total = total + r1[i].astype(F32)
    z2[...] = total.astype(BF16)
    r2[seg] = z2[...]

    def segment_step(d, carry):
        remote(
            z2, r2.at[seg], ar_send.at[1], ar_recv.at[1], (g, (z + SEG * d) % NZ)
        ).start()
        return carry

    lax.fori_loop(1, NSEG, segment_step, 0)
    exchange(3, gs, gr, 16, NZ - 1, False)

    exchange_wait(2, or_, True)
    out_ref[...] = dot(pts[...], rows_of(or_).astype(BF16), 1, 0).astype(BF16)

    three = r2.at[pl.ds(0, NSEG - 1)]
    remote(three, three, ar_send.at[1], ar_recv.at[1], partner).wait_recv()
    total = r2[0].astype(F32)
    for i in range(1, NSEG):
        total = total + r2[i].astype(F32)
    z3[...] = total.astype(BF16)
    r3[idx] = z3[...]

    def share_step(d, carry):
        i, dev = in_segment(d)
        remote(z3, r3.at[idx], ar_send.at[2], ar_recv.at[2], dev).start()
        return carry

    lax.fori_loop(1, SEG, share_step, 0)
    eight = r3.at[pl.ds(0, SEG - 1)]
    last = remote(eight, eight, ar_send.at[2], ar_recv.at[2], partner)
    last.wait_recv()
    for k in range(40):
        j, r = k // 2, k % 2
        tile = r3[k // 5, k % 5].astype(F32)
        if j < 16:
            gu_ref[8 * r : 8 * r + 8, 128 * j : 128 * j + 128] = tile
        else:
            go_ref[8 * r : 8 * r + 8, 128 * (j - 16) : 128 * (j - 15)] = tile

    exchange_wait(3, gr, True)
    grad_ref[...] = dot(pts[...], rows_of(gr).astype(BF16), 1, 0).astype(BF16)

    for which, buf in enumerate((xs, cs, os_, gs)):
        exchange_wait(which, buf, False)
    for copy in (w_x0, w_x1, w_x2, w_x3, w_y0, w_y1, w_y2, w_y3, w_c, p_c):
        copy.wait_send()
    for copies in (ca, cb, ca2, cb2):
        for copy in copies:
            copy.wait_send()
    remote(seven, seven, ar_send.at[0], ar_recv.at[0], partner).wait_send()
    remote(three, three, ar_send.at[1], ar_recv.at[1], partner).wait_send()
    last.wait_send()


def on_device(inputs, cotangent, w_uvqk, w_out, send_perm, recv_perm, lengths, prefixes):
    vmem = pl.BlockSpec(memory_space=pltpu.VMEM)
    smem = pl.BlockSpec(memory_space=pltpu.SMEM)
    blocks = pltpu.VMEM((BLK, BLOCK, D), BF16)

    def buf(*shape, dtype=BF16):
        return pltpu.VMEM(shape, dtype)

    dma = pltpu.SemaphoreType.DMA
    out, grad, gu, go = pl.pallas_call(
        kernel,
        out_shape=(
            jax.ShapeDtypeStruct((ROWS, D), BF16),
            jax.ShapeDtypeStruct((ROWS, D), BF16),
            jax.ShapeDtypeStruct((16, 4 * D), F32),
            jax.ShapeDtypeStruct((16, D), F32),
        ),
        in_specs=[vmem] * 4 + [smem] * 4,
        out_specs=(vmem,) * 4,
        scratch_shapes=[
            *([blocks] * 8),
            buf(4, 4, 2, 16, COLS),
            buf(4, 4, 2, 16, COLS),
            buf(4, 4, 16, COLS),
            buf(4, 2, 2, 16, HALF),
            buf(4, 2, 2, 16, HALF),
            buf(4, 2, 16, QUART),
            buf(4, 2, 16, QUART),
            buf(2, 2, 16, HALF),
            buf(2, 2, 16, HALF),
            buf(2, 16, QUART),
            buf(2, 16, QUART),
            buf(2, 2, 2, 16, HALF),
            buf(2, 2, 2, 16, HALF),
            buf(2, 2, 16, QUART),
            buf(2, 2, 16, QUART),
            buf(SEG, 5, 8, 128),
            buf(SEG, 5, 8, 128),
            buf(5, 8, 128),
            buf(NSEG, 5, 8, 128),
            buf(5, 8, 128),
            buf(SEG, 5, 8, 128),
            buf(ROWS, ROWS),
            buf(ROWS, ROWS),
            buf(ROWS, ROWS, dtype=F32),
            buf(ROWS, D, dtype=F32),
            buf(ROWS, D, dtype=F32),
            buf(ROWS, 128, dtype=F32),
            buf(ROWS, D),
            buf(ROWS, 4 * D),
            buf(ROWS, 4 * D, dtype=F32),
            buf(ROWS, D, dtype=F32),
            buf(ROWS, D),
            buf(ROWS, 4 * D),
            buf(HEADS, ROWS, ROWS),
            buf(HEADS, ROWS, ROWS, dtype=F32),
            dma((4,)),
            dma((4,)),
            dma((9,)),
            dma((9,)),
            dma((25,)),
            dma((25,)),
            dma((3,)),
            dma((3,)),
        ],
        compiler_params=pltpu.CompilerParams(
            collective_id=0, has_side_effects=True, vmem_limit_bytes=60 * 1024 * 1024
        ),
    )(
        inputs[0],
        cotangent[0],
        w_uvqk,
        w_out,
        send_perm[0, 0],
        recv_perm[0, 0],
        lengths[0, 0],
        prefixes[0, 0],
    )
    return (out[None], grad[None], gu, go)


def solution(mesh):
    rows = P("group", "shuf", None)
    return jax.shard_map(
        on_device,
        mesh=mesh,
        in_specs=(rows, rows, P("group", None), P("group", None), rows, rows, rows, rows),
        out_specs=(rows, rows, P("group", None), P("group", None)),
        check_vma=False,
    )
```

```python
import jax
import jax.numpy as jnp
from jax import lax
from jax.experimental import pallas as pl
from jax.experimental.pallas import tpu as pltpu
from jax.sharding import PartitionSpec as P

D = 512
HEADS = 8
ROWS = 256
BLOCK = 8
BLK = 32
USERS = 8
NZ = 32
SEG = 8
NSEG = 4
COLS = 2560
HALF = 1280
EPS = 1e-05
MESH = pl.DeviceIdType.MESH
F32 = jnp.float32
BF16 = jnp.bfloat16


def dot(a, b, ca, cb):
    return lax.dot_general(a, b, (((ca,), (cb,)), ((), ())), preferred_element_type=F32)


def kernel(
    x_in, c_in, wu_in, wo_in, sp_in, rp_in, len_in, pre_in,
    or_, gr, r3,
    xs, xr, cs, cr, os_, gs,
    wfull, pb, rc, sa, sb, sa2, sb2, ta, tb, ta2, tb2, ua, ub, ua2, ub2,
    z1, r1, z2, r2, z3,
    pts, ptr, vis, xf, zf, inv, xn, act, dact, mixed, gated, gproj, w8, d8,
    meet, a2a_send, a2a_recv, ag_send, ag_recv, rs_send, rs_recv, ar_send, ar_recv,
):
    g = lax.axis_index("group")
    z = lax.axis_index("shuf")
    core = g % 2
    xx = (g // 2) % 4
    yy = g // 8

    def gid(y, x, c):
        return (y * 4 + x) * 2 + c

    xplus = (gid(yy, (xx + 1) % 4, core), z)
    xminus = (gid(yy, (xx + 3) % 4, core), z)
    yplus = (gid((yy + 1) % 4, xx, core), z)
    yminus = (gid((yy + 3) % 4, xx, core), z)
    partner = (gid(yy, xx, 1 - core), z)

    def remote(src, dst, ssem, rsem, dev):
        return pltpu.make_async_remote_copy(
            src_ref=src, dst_ref=dst, send_sem=ssem, recv_sem=rsem,
            device_id=dev, device_id_type=MESH,
        )

    barrier = pltpu.get_barrier_semaphore()
    for dev in (xplus, xminus, yplus, yminus, partner):
        pl.semaphore_signal(barrier, inc=1, device_id=dev, device_id_type=MESH)

    def up_down(d):
        return (g, (z + d) % NZ), (g, (z + NZ - d) % NZ)

    for d in range(1, 5):
        for dev in up_down(d):
            pl.semaphore_signal(barrier, inc=1, device_id=dev, device_id_type=MESH)

    def meet_open(i, d):
        for dev in up_down(d):
            pl.semaphore_signal(meet.at[i], inc=1, device_id=dev, device_id_type=MESH)

    lane = lax.broadcasted_iota(jnp.int32, (1, ROWS), 1)
    row_of = lax.broadcasted_iota(jnp.int32, (ROWS, ROWS), 0)

    def one_hot(perm_ref):
        index = lane % BLOCK
        for t in range(BLK):
            index = index + jnp.where(lane // BLOCK == t, perm_ref[t] * BLOCK, 0)
        return (row_of == index).astype(F32).astype(BF16)

    def to_blocks(value):
        return value.reshape(BLK, BLOCK, D).astype(BF16)

    def rows_of(ref):
        return ref[...].astype(F32).reshape(ROWS, D)

    wfull[yy, xx, core, :, 0 : 4 * D] = wu_in[...]
    wfull[yy, xx, core, :, 4 * D : COLS] = wo_in[...]
    pts[...] = one_hot(sp_in)
    xs[...] = to_blocks(dot(pts[...], x_in[...], 0, 0))
    cs[...] = to_blocks(dot(pts[...], c_in[...], 0, 0))

    def exchange(which, src, dst, first, last, far):
        def step(i, carry):
            k = NZ - 2 - i if far else i
            peer = (z + NZ + (k // 2 + 1) * (1 - 2 * (k % 2))) % NZ
            remote(
                src.at[peer], dst.at[z], a2a_send.at[which], a2a_recv.at[which], (g, peer)
            ).start()
            return carry

        lax.fori_loop(first, last, step, 0)

    def exchange_wait(which, buf, recv):
        part = buf.at[pl.ds(0, NZ - 1)]
        copy = remote(
            part, part, a2a_send.at[which], a2a_recv.at[which], (g, (z + 1) % NZ)
        )
        if recv:
            copy.wait_recv()
        else:
            copy.wait_send()

    pl.semaphore_wait(barrier, 5 + 8)
    meet_open(0, 4)
    exchange(0, xs, xr, 0, 8, False)

    def gather(i, part, dev):
        copy = remote(part, part, ag_send.at[i], ag_recv.at[i], dev)
        copy.start()
        return copy

    def half_x(x, h):
        return wfull.at[yy, x, core, :, pl.ds(h * HALF, HALF)]

    def half_y(y, h):
        return wfull.at[y, pl.ds(2 * h, 2), core]

    own = wfull.at[yy, xx, core]
    w_x0 = gather(0, own, xplus)
    w_x1 = gather(1, own, xminus)
    exchange(1, cs, cr, 0, 8, False)
    ptr[...] = one_hot(rp_in)
    xr[z] = xs[z]
    cr[z] = cs[z]
    pl.semaphore_wait(meet.at[0], 2)
    meet_open(1, 8)
    exchange(0, xs, xr, 8, 16, False)
    exchange(1, cs, cr, 8, 16, False)
    ri = lax.broadcasted_iota(jnp.int32, (ROWS, 1), 0)
    uid_r = jnp.zeros((ROWS, 1), jnp.int32)
    uid_k = jnp.zeros((1, ROWS), jnp.int32)
    pre_r = jnp.zeros((ROWS, 1), jnp.int32) + pre_in[0]
    start_k = jnp.zeros((1, ROWS), jnp.int32)
    end = len_in[0]
    for u in range(USERS):
        past_r = ri >= end
        past_k = lane >= end
        uid_r = uid_r + jnp.where(past_r, 1, 0)
        uid_k = uid_k + jnp.where(past_k, 1, 0)
        start_k = start_k + jnp.where(past_k, len_in[u], 0)
        if u < USERS - 1:
            pre_r = pre_r + jnp.where(past_r, pre_in[u + 1] - pre_in[u], 0)
            end = end + len_in[u + 1]
    allowed = jnp.where(
        uid_r == uid_k,
        jnp.where(lane <= ri, 1.0, jnp.where(lane - start_k < pre_r, 1.0, 0.0)),
        0.0,
    )
    vis[...] = allowed * (1.0 / ROWS)

    w_x0.wait_recv()
    w_x2 = gather(2, half_x((xx + 3) % 4, 0), xplus)
    w_x1.wait_recv()
    w_x3 = gather(3, half_x((xx + 1) % 4, 1), xminus)
    w_x2.wait_recv()
    w_x3.wait_recv()
    mine = wfull.at[yy, :, core]
    w_y0 = gather(4, mine, yplus)
    w_y1 = gather(5, mine, yminus)
    w_c = [gather(8, mine, partner)]
    pl.semaphore_wait(meet.at[1], 2)
    exchange(0, xs, xr, 0, 15, True)
    exchange(1, cs, cr, 0, 15, True)
    w_y0.wait_recv()
    w_y2 = gather(6, half_y((yy + 3) % 4, 0), yplus)
    w_y1.wait_recv()
    w_y3 = gather(7, half_y((yy + 1) % 4, 1), yminus)
    w_c.append(gather(9, wfull.at[(yy + 3) % 4, :, core], partner))
    w_c.append(gather(10, wfull.at[(yy + 1) % 4, :, core], partner))
    w_y2.wait_recv()
    w_y3.wait_recv()
    w_c.append(gather(11, wfull.at[(yy + 2) % 4, :, core], partner))

    exchange_wait(0, xr, True)
    x32 = dot(ptr[...], rows_of(xr).astype(BF16), 0, 0)
    xf[...] = x32
    center = jnp.mean(x32, axis=-1, keepdims=True)
    centred = x32 - center
    scale = lax.rsqrt(jnp.mean(centred * centred, axis=-1, keepdims=True) + EPS)
    inv[...] = jnp.broadcast_to(scale, (ROWS, 128))
    normed_x = centred * scale
    zf[...] = normed_x
    xn[...] = normed_x.astype(BF16)
    for copy in w_c:
        copy.wait_recv()

    def weight(c):
        return wfull[:, :, :, :, pl.ds(pl.multiple_of(c * D, D), D)].reshape(D, D)

    def project(c, carry):
        cols = pl.ds(pl.multiple_of(c * D, D), D)
        p = dot(xn[...], weight(c), 1, 0)
        s = jax.nn.sigmoid(p)
        act[:, cols] = (p * s).astype(BF16)
        dact[:, cols] = s * (1.0 + p * (1.0 - s))
        return carry

    lax.fori_loop(0, 4, project, 0)

    lane128 = lax.broadcasted_iota(jnp.int32, (ROWS, 128), 1)

    def pair_cols(base, p):
        return pl.ds(pl.multiple_of(base * D + p * 128, 128), 128)

    def attend(p, carry):
        v = act[:, pair_cols(1, p)]
        q = act[:, pair_cols(2, p)].astype(F32)
        k = act[:, pair_cols(3, p)]
        parts = []
        for h in range(2):
            inside = (lane128 // 64) == h
            qh = jnp.where(inside, q, 0.0).astype(BF16)
            scores = dot(qh, k, 1, 1)
            s = jax.nn.sigmoid(scores)
            allow = vis[...]
            wts = (scores * s * allow).astype(BF16)
            w8[2 * p + h] = wts
            d8[2 * p + h] = s * (1.0 + scores * (1.0 - s)) * allow
            parts.append(dot(wts, v, 1, 0))
        mixed[:, pl.ds(pl.multiple_of(p * 128, 128), 128)] = jnp.where(
            lane128 < 64, parts[0], parts[1]
        )
        return carry

    lax.fori_loop(0, HEADS // 2, attend, 0)

    m32 = mixed[...]
    m_center = jnp.mean(m32, axis=-1, keepdims=True)
    m_centred = m32 - m_center
    m_scale = lax.rsqrt(jnp.mean(m_centred * m_centred, axis=-1, keepdims=True) + EPS)
    m_normed = m_centred * m_scale
    mixed[...] = m_normed
    gated[...] = (m_normed * act[:, 0:D].astype(F32)).astype(BF16)
    layer = (dot(gated[...], weight(4), 1, 0) + xf[...]).astype(BF16)
    os_[...] = to_blocks(dot(ptr[...], layer, 1, 0))
    or_[z] = os_[z]
    exchange(2, os_, or_, 0, NZ - 1, True)

    exchange_wait(1, cr, True)
    cot = dot(ptr[...], rows_of(cr).astype(BF16), 0, 0)
    cot16 = cot.astype(BF16)
    xf[...] = cot
    p_c = [
        remote(pb.at[c, :, :, 1 - core], rc.at[c], rs_send.at[24 + c], rs_recv.at[24 + c], partner)
        for c in range(5)
    ]
    pb[4] = dot(gated[...], cot16, 0, 0).astype(BF16).reshape(4, 4, 2, 16, D)
    p_c[4].start()

    def weight_grad(c):
        part = dot(xn[...], gproj[:, c * D : (c + 1) * D], 0, 0)
        pb[c] = part.astype(BF16).reshape(4, 4, 2, 16, D)
        p_c[c].start()

    g_gated = dot(cot16, weight(4), 1, 1).astype(BF16).astype(F32)
    m_normed = mixed[...]
    g_normed = g_gated * act[:, 0:D].astype(F32)
    g_u = (g_gated * m_normed).astype(BF16).astype(F32)
    gproj[:, 0:D] = (g_u * dact[:, 0:D]).astype(BF16)
    weight_grad(0)
    g_mixed = m_scale * (
        g_normed
        - jnp.mean(g_normed, axis=-1, keepdims=True)
        - m_normed * jnp.mean(g_normed * m_normed, axis=-1, keepdims=True)
    )
    gated[...] = g_mixed.astype(BF16)

    def attend_back(p, carry):
        v = act[:, pair_cols(1, p)]
        q = act[:, pair_cols(2, p)]
        k = act[:, pair_cols(3, p)]
        gm = gated[:, pl.ds(pl.multiple_of(p * 128, 128), 128)]
        gv, gq, gk = [], [], []
        for h in range(2):
            inside = (lane128 // 64) == h
            gmh = jnp.where(inside, gm.astype(F32), 0.0).astype(BF16)
            g_w = dot(gmh, v, 1, 1).astype(BF16).astype(F32)
            g_s = (g_w * d8[2 * p + h]).astype(BF16)
            gv.append(dot(w8[2 * p + h], gm, 0, 0))
            gq.append(dot(g_s, k, 1, 0))
            gk.append(dot(g_s, q, 0, 0))
        for base, part in ((1, gv), (2, gq), (3, gk)):
            value = jnp.where(lane128 < 64, part[0], part[1]).astype(BF16).astype(F32)
            cols = pair_cols(base, p)
            gproj[:, cols] = (value * dact[:, cols]).astype(BF16)
        return carry

    lax.fori_loop(0, HEADS // 2, attend_back, 0)

    for c in range(1, 4):
        weight_grad(c)

    mixed[...] = dot(gproj[:, 0:D], weight(0), 1, 1)

    def input_grad(c, carry):
        cols = pl.ds(pl.multiple_of(c * D, D), D)
        mixed[...] = mixed[...] + dot(gproj[:, cols], weight(c), 1, 1)
        return carry

    lax.fori_loop(1, 4, input_grad, 0)
    def core_sum(c):
        def step(i, carry):
            y = i // 4
            x = i % 4
            total = (pb[c, y, x, core].astype(F32) + rc[c, y, x].astype(F32)).astype(BF16)
            sa[y, x // 2, x % 2, :, c * D : (c + 1) * D] = total[0:8]
            sb[x, y // 2, y % 2, :, c * D : (c + 1) * D] = total[8:16]
            return carry

        lax.fori_loop(0, 16, step, 0)

    for c in (4, 0, 1, 2, 3):
        p_c[c].wait_recv()
        core_sum(c)

    def ring_open(base, me, plus, minus, s, t, u):
        opp, nxt, prv = (me + 2) % 4, (me + 1) % 4, (me + 3) % 4
        plan = (
            (s.at[opp, 0], t.at[0], plus),
            (s.at[opp, 1], t.at[1], minus),
            (s.at[nxt, 1], u.at[0, 1], plus),
            (s.at[prv, 0], u.at[1, 0], minus),
            (s.at[nxt, 0], u.at[0, 0], plus),
            (s.at[prv, 1], u.at[1, 1], minus),
        )
        copies = [
            remote(src, dst, rs_send.at[base + i], rs_recv.at[base + i], dev)
            for i, (src, dst, dev) in enumerate(plan)
        ]
        for copy in copies[:4]:
            copy.start()
        return copies

    def ring_pass(copies, me, s, t):
        nxt, prv = (me + 1) % 4, (me + 3) % 4
        copies[0].wait_recv()
        s[nxt, 0] = (s[nxt, 0].astype(F32) + t[0].astype(F32)).astype(BF16)
        copies[4].start()
        copies[1].wait_recv()
        s[prv, 1] = (s[prv, 1].astype(F32) + t[1].astype(F32)).astype(BF16)
        copies[5].start()

    def ring_close(copies, me, s, u, h):
        return s[me, h].astype(F32) + u[0, h].astype(F32) + u[1, h].astype(F32)

    ca = ring_open(0, yy, yplus, yminus, sa, ta, ua)
    cb = ring_open(6, xx, xplus, xminus, sb, tb, ub)
    g_xn = mixed[...]
    zz = zf[...]
    g_x = inv[:, 0:1] * (
        g_xn
        - jnp.mean(g_xn, axis=-1, keepdims=True)
        - zz * jnp.mean(g_xn * zz, axis=-1, keepdims=True)
    ) + xf[...]
    gs[...] = to_blocks(dot(ptr[...], g_x.astype(BF16), 1, 0))
    gr[z] = gs[z]
    exchange(3, gs, gr, 0, 11, True)
    ring_pass(ca, yy, sa, ta)
    ring_pass(cb, xx, sb, tb)
    for copies in (ca, cb):
        for i in range(2, 6):
            copies[i].wait_recv()
    for h in range(2):
        total = ring_close(ca, yy, sa, ua, h).astype(BF16)
        for i in range(2):
            for q in range(2):
                sa2[2 * h + i, q] = total[i, :, q * HALF : (q + 1) * HALF]
    for h in range(2):
        total = ring_close(cb, xx, sb, ub, h).astype(BF16)
        for i in range(2):
            for q in range(2):
                sb2[2 * h + i, q] = total[i, :, q * HALF : (q + 1) * HALF]
    ca2 = ring_open(12, xx, xplus, xminus, sa2, ta2, ua2)
    cb2 = ring_open(18, yy, yplus, yminus, sb2, tb2, ub2)
    ring_pass(ca2, xx, sa2, ta2)
    ring_pass(cb2, yy, sb2, tb2)
    for copies in (ca2, cb2):
        for i in range(2, 6):
            copies[i].wait_recv()
    for which, (copies, me, s, u) in enumerate(((ca2, xx, sa2, ua2), (cb2, yy, sb2, ub2))):
        for h in range(2):
            total = ring_close(copies, me, s, u, h)
            for j in range(10):
                k = (h * 10 + j) * 2 + which
                z1[k // 5, k % 5] = total[:, 128 * j : 128 * j + 128].astype(BF16)

    seg = z // SEG
    idx = z % SEG

    def in_segment(d):
        i = (idx + d) % SEG
        return i, (g, seg * SEG + i)

    def scatter_step(d, carry):
        i, dev = in_segment(d)
        remote(z1.at[i], r1.at[idx], ar_send.at[0], ar_recv.at[0], dev).start()
        return carry

    lax.fori_loop(1, SEG, scatter_step, 0)
    exchange(3, gs, gr, 11, 17, True)
    r1[idx] = z1[idx]
    seven = r1.at[pl.ds(0, SEG - 1)]
    remote(seven, seven, ar_send.at[0], ar_recv.at[0], partner).wait_recv()
    total = r1[0].astype(F32)
    for i in range(1, SEG):
        total = total + r1[i].astype(F32)
    z2[...] = total.astype(BF16)
    r2[seg] = z2[...]

    def segment_step(d, carry):
        remote(
            z2, r2.at[seg], ar_send.at[1], ar_recv.at[1], (g, (z + SEG * d) % NZ)
        ).start()
        return carry

    lax.fori_loop(1, NSEG, segment_step, 0)
    exchange(3, gs, gr, 17, 25, True)

    three = r2.at[pl.ds(0, NSEG - 1)]
    remote(three, three, ar_send.at[1], ar_recv.at[1], partner).wait_recv()
    total = r2[0].astype(F32)
    for i in range(1, NSEG):
        total = total + r2[i].astype(F32)
    z3[...] = total.astype(BF16)
    r3[idx] = z3[...]

    def share_step(d, carry):
        i, dev = in_segment(d)
        remote(z3, r3.at[idx], ar_send.at[2], ar_recv.at[2], dev).start()
        return carry

    lax.fori_loop(1, SEG, share_step, 0)
    exchange(3, gs, gr, 25, NZ - 1, True)
    exchange_wait(2, or_, True)
    eight = r3.at[pl.ds(0, SEG - 1)]
    last = remote(eight, eight, ar_send.at[2], ar_recv.at[2], partner)
    last.wait_recv()
    exchange_wait(3, gr, True)

    for which, buf in enumerate((xs, cs, os_, gs)):
        exchange_wait(which, buf, False)
    for copy in (w_x0, w_x1, w_x2, w_x3, w_y0, w_y1, w_y2, w_y3, *w_c, *p_c):
        copy.wait_send()
    for copies in (ca, cb, ca2, cb2):
        for copy in copies:
            copy.wait_send()
    remote(seven, seven, ar_send.at[0], ar_recv.at[0], partner).wait_send()
    remote(three, three, ar_send.at[1], ar_recv.at[1], partner).wait_send()
    last.wait_send()


def finish(or_ref, gr_ref, sum_ref, sp_in, out_ref, grad_ref, gu_ref, go_ref):
    lane = lax.broadcasted_iota(jnp.int32, (1, ROWS), 1)
    index = lane % BLOCK
    for t in range(BLK):
        index = index + jnp.where(lane // BLOCK == t, sp_in[t] * BLOCK, 0)
    hot = lax.broadcasted_iota(jnp.int32, (ROWS, ROWS), 0) == index
    hot = hot.astype(F32).astype(BF16)
    for src, dst in ((or_ref, out_ref), (gr_ref, grad_ref)):
        rows = src[...].astype(F32).reshape(ROWS, D).astype(BF16)
        dst[...] = dot(hot, rows, 1, 0).astype(BF16)
    for k in range(40):
        j, r = k // 2, k % 2
        tile = sum_ref[k // 5, k % 5].astype(F32)
        if j < 16:
            gu_ref[8 * r : 8 * r + 8, 128 * j : 128 * j + 128] = tile
        else:
            go_ref[8 * r : 8 * r + 8, 128 * (j - 16) : 128 * (j - 15)] = tile


def on_device(inputs, cotangent, w_uvqk, w_out, send_perm, recv_perm, lengths, prefixes):
    vmem = pl.BlockSpec(memory_space=pltpu.VMEM)
    smem = pl.BlockSpec(memory_space=pltpu.SMEM)
    blocks = pltpu.VMEM((BLK, BLOCK, D), BF16)

    def buf(*shape, dtype=BF16):
        return pltpu.VMEM(shape, dtype)

    dma = pltpu.SemaphoreType.DMA
    send_order = send_perm[0, 0]
    back_out, back_grad, sums = pl.pallas_call(
        kernel,
        out_shape=(
            jax.ShapeDtypeStruct((BLK, BLOCK, D), BF16),
            jax.ShapeDtypeStruct((BLK, BLOCK, D), BF16),
            jax.ShapeDtypeStruct((SEG, 5, 8, 128), BF16),
        ),
        in_specs=[vmem] * 4 + [smem] * 4,
        out_specs=(vmem,) * 3,
        scratch_shapes=[
            *([blocks] * 6),
            buf(4, 4, 2, 16, COLS),
            buf(5, 4, 4, 2, 16, D),
            buf(5, 4, 4, 16, D),
            buf(4, 2, 2, 8, COLS),
            buf(4, 2, 2, 8, COLS),
            buf(4, 2, 8, HALF),
            buf(4, 2, 8, HALF),
            buf(2, 2, 8, COLS),
            buf(2, 2, 8, COLS),
            buf(2, 8, HALF),
            buf(2, 8, HALF),
            buf(2, 2, 2, 8, COLS),
            buf(2, 2, 2, 8, COLS),
            buf(2, 2, 8, HALF),
            buf(2, 2, 8, HALF),
            buf(SEG, 5, 8, 128),
            buf(SEG, 5, 8, 128),
            buf(5, 8, 128),
            buf(NSEG, 5, 8, 128),
            buf(5, 8, 128),
            buf(ROWS, ROWS),
            buf(ROWS, ROWS),
            buf(ROWS, ROWS, dtype=F32),
            buf(ROWS, D, dtype=F32),
            buf(ROWS, D, dtype=F32),
            buf(ROWS, 128, dtype=F32),
            buf(ROWS, D),
            buf(ROWS, 4 * D),
            buf(ROWS, 4 * D, dtype=F32),
            buf(ROWS, D, dtype=F32),
            buf(ROWS, D),
            buf(ROWS, 4 * D),
            buf(HEADS, ROWS, ROWS),
            buf(HEADS, ROWS, ROWS, dtype=F32),
            pltpu.SemaphoreType.REGULAR((2,)),
            dma((4,)),
            dma((4,)),
            dma((12,)),
            dma((12,)),
            dma((29,)),
            dma((29,)),
            dma((3,)),
            dma((3,)),
        ],
        compiler_params=pltpu.CompilerParams(
            collective_id=0, has_side_effects=True, vmem_limit_bytes=60 * 1024 * 1024
        ),
    )(
        inputs[0],
        cotangent[0],
        w_uvqk,
        w_out,
        send_order,
        recv_perm[0, 0],
        lengths[0, 0],
        prefixes[0, 0],
    )
    out, grad, gu, go = pl.pallas_call(
        finish,
        out_shape=(
            jax.ShapeDtypeStruct((ROWS, D), BF16),
            jax.ShapeDtypeStruct((ROWS, D), BF16),
            jax.ShapeDtypeStruct((16, 4 * D), F32),
            jax.ShapeDtypeStruct((16, D), F32),
        ),
        in_specs=[vmem] * 3 + [smem],
        out_specs=(vmem,) * 4,
    )(back_out, back_grad, sums, send_order)
    return (out[None], grad[None], gu, go)


def solution(mesh):
    rows = P("group", "shuf", None)
    return jax.shard_map(
        on_device,
        mesh=mesh,
        in_specs=(rows, rows, P("group", None), P("group", None), rows, rows, rows, rows),
        out_specs=(rows, rows, P("group", None), P("group", None)),
        check_vma=False,
    )
```

```python
import jax
import jax.numpy as jnp
from jax import lax
from jax.experimental import pallas as pl
from jax.experimental.pallas import tpu as pltpu
from jax.sharding import PartitionSpec as P

D = 512
HEADS = 8
ROWS = 256
BLOCK = 8
BLK = 32
USERS = 8
NZ = 32
SEG = 8
NSEG = 4
COLS = 2560
HALF = 1280
EPS = 1e-05
MESH = pl.DeviceIdType.MESH
F32 = jnp.float32
BF16 = jnp.bfloat16


def dot(a, b, ca, cb):
    return lax.dot_general(a, b, (((ca,), (cb,)), ((), ())), preferred_element_type=F32)


def kernel(
    x_in, c_in, wu_in, wo_in, sp_in, rp_in, len_in, pre_in,
    or_, gr, r3,
    xs, xr, cs, cr, os_, gs,
    wfull, pb, rc, sa, sb, sa2, sb2, ta, tb, ta2, tb2, ua, ub, ua2, ub2,
    z1, r1, z2, r2, z3, x_buf, c_buf, load_sem,
    pts, ptr, vis, xf, zf, inv, xn, act, dact, mixed, gated, gproj, w8, d8,
    meet, a2a_send, a2a_recv, ag_send, ag_recv, rs_send, rs_recv, ar_send, ar_recv,
):
    g = lax.axis_index("group")
    z = lax.axis_index("shuf")
    core = g % 2
    xx = (g // 2) % 4
    yy = g // 8

    def gid(y, x, c):
        return (y * 4 + x) * 2 + c

    xplus = (gid(yy, (xx + 1) % 4, core), z)
    xminus = (gid(yy, (xx + 3) % 4, core), z)
    yplus = (gid((yy + 1) % 4, xx, core), z)
    yminus = (gid((yy + 3) % 4, xx, core), z)
    partner = (gid(yy, xx, 1 - core), z)

    def remote(src, dst, ssem, rsem, dev):
        return pltpu.make_async_remote_copy(
            src_ref=src, dst_ref=dst, send_sem=ssem, recv_sem=rsem,
            device_id=dev, device_id_type=MESH,
        )

    own = wfull.at[yy, xx, core]
    loads = [
        pltpu.make_async_copy(src, dst, load_sem.at[i])
        for i, (src, dst) in enumerate(
            (
                (x_in, x_buf),
                (c_in, c_buf),
                (wu_in, own.at[:, pl.ds(0, 4 * D)]),
                (wo_in, own.at[:, pl.ds(4 * D, D)]),
            )
        )
    ]

    barrier = pltpu.get_barrier_semaphore()
    for dev in (xplus, xminus, yplus, yminus, partner):
        pl.semaphore_signal(barrier, inc=1, device_id=dev, device_id_type=MESH)

    for copy in loads:
        copy.start()

    def up_down(d):
        return (g, (z + d) % NZ), (g, (z + NZ - d) % NZ)

    for d in range(1, 5):
        for dev in up_down(d):
            pl.semaphore_signal(barrier, inc=1, device_id=dev, device_id_type=MESH)

    def meet_open(i, d):
        for dev in up_down(d):
            pl.semaphore_signal(meet.at[i], inc=1, device_id=dev, device_id_type=MESH)

    lane = lax.broadcasted_iota(jnp.int32, (1, ROWS), 1)
    row_of = lax.broadcasted_iota(jnp.int32, (ROWS, ROWS), 0)

    def one_hot(perm_ref):
        index = lane % BLOCK
        for t in range(BLK):
            index = index + jnp.where(lane // BLOCK == t, perm_ref[t] * BLOCK, 0)
        return (row_of == index).astype(F32).astype(BF16)

    def to_blocks(value):
        return value.reshape(BLK, BLOCK, D).astype(BF16)

    def rows_of(ref):
        return ref[...].astype(F32).reshape(ROWS, D)

    pts[...] = one_hot(sp_in)
    loads[0].wait()
    xs[...] = to_blocks(dot(pts[...], x_buf[...], 0, 0))
    loads[1].wait()
    cs[...] = to_blocks(dot(pts[...], c_buf[...], 0, 0))
    loads[2].wait()
    loads[3].wait()

    def exchange(which, src, dst, first, last, far):
        def step(i, carry):
            k = NZ - 2 - i if far else i
            peer = (z + NZ + (k // 2 + 1) * (1 - 2 * (k % 2))) % NZ
            remote(
                src.at[peer], dst.at[z], a2a_send.at[which], a2a_recv.at[which], (g, peer)
            ).start()
            return carry

        lax.fori_loop(first, last, step, 0)

    def exchange_wait(which, buf, recv):
        part = buf.at[pl.ds(0, NZ - 1)]
        copy = remote(
            part, part, a2a_send.at[which], a2a_recv.at[which], (g, (z + 1) % NZ)
        )
        if recv:
            copy.wait_recv()
        else:
            copy.wait_send()

    pl.semaphore_wait(barrier, 5 + 8)
    meet_open(0, 4)
    exchange(0, xs, xr, 0, 8, False)

    def gather(i, part, dev):
        copy = remote(part, part, ag_send.at[i], ag_recv.at[i], dev)
        copy.start()
        return copy

    def half_x(x, h):
        return wfull.at[yy, x, core, :, pl.ds(h * HALF, HALF)]

    def half_y(y, h):
        return wfull.at[y, pl.ds(2 * h, 2), core]

    w_x0 = gather(0, own, xplus)
    w_x1 = gather(1, own, xminus)
    exchange(1, cs, cr, 0, 8, False)
    ptr[...] = one_hot(rp_in)
    xr[z] = xs[z]
    cr[z] = cs[z]
    pl.semaphore_wait(meet.at[0], 2)
    meet_open(1, 8)
    exchange(0, xs, xr, 8, 16, False)
    exchange(1, cs, cr, 8, 16, False)
    ri = lax.broadcasted_iota(jnp.int32, (ROWS, 1), 0)
    uid_r = jnp.zeros((ROWS, 1), jnp.int32)
    uid_k = jnp.zeros((1, ROWS), jnp.int32)
    pre_r = jnp.zeros((ROWS, 1), jnp.int32) + pre_in[0]
    start_k = jnp.zeros((1, ROWS), jnp.int32)
    end = len_in[0]
    for u in range(USERS):
        past_r = ri >= end
        past_k = lane >= end
        uid_r = uid_r + jnp.where(past_r, 1, 0)
        uid_k = uid_k + jnp.where(past_k, 1, 0)
        start_k = start_k + jnp.where(past_k, len_in[u], 0)
        if u < USERS - 1:
            pre_r = pre_r + jnp.where(past_r, pre_in[u + 1] - pre_in[u], 0)
            end = end + len_in[u + 1]
    allowed = jnp.where(
        uid_r == uid_k,
        jnp.where(lane <= ri, 1.0, jnp.where(lane - start_k < pre_r, 1.0, 0.0)),
        0.0,
    )
    vis[...] = allowed * (1.0 / ROWS)

    w_x0.wait_recv()
    w_x2 = gather(2, half_x((xx + 3) % 4, 0), xplus)
    w_x1.wait_recv()
    w_x3 = gather(3, half_x((xx + 1) % 4, 1), xminus)
    w_x2.wait_recv()
    w_x3.wait_recv()
    mine = wfull.at[yy, :, core]
    w_y0 = gather(4, mine, yplus)
    w_y1 = gather(5, mine, yminus)
    w_c = [gather(8, mine, partner)]
    pl.semaphore_wait(meet.at[1], 2)
    exchange(0, xs, xr, 0, 15, True)
    exchange(1, cs, cr, 0, 15, True)
    w_y0.wait_recv()
    w_y2 = gather(6, half_y((yy + 3) % 4, 0), yplus)
    w_y1.wait_recv()
    w_y3 = gather(7, half_y((yy + 1) % 4, 1), yminus)
    w_c.append(gather(9, wfull.at[(yy + 3) % 4, :, core], partner))
    w_c.append(gather(10, wfull.at[(yy + 1) % 4, :, core], partner))
    w_y2.wait_recv()
    w_y3.wait_recv()
    w_c.append(gather(11, wfull.at[(yy + 2) % 4, :, core], partner))

    exchange_wait(0, xr, True)
    x32 = dot(ptr[...], rows_of(xr).astype(BF16), 0, 0)
    xf[...] = x32
    center = jnp.mean(x32, axis=-1, keepdims=True)
    centred = x32 - center
    scale = lax.rsqrt(jnp.mean(centred * centred, axis=-1, keepdims=True) + EPS)
    inv[...] = jnp.broadcast_to(scale, (ROWS, 128))
    normed_x = centred * scale
    zf[...] = normed_x
    xn[...] = normed_x.astype(BF16)
    for copy in w_c:
        copy.wait_recv()

    def weight(c):
        return wfull[:, :, :, :, pl.ds(pl.multiple_of(c * D, D), D)].reshape(D, D)

    def project(c, carry):
        cols = pl.ds(pl.multiple_of(c * D, D), D)
        p = dot(xn[...], weight(c), 1, 0)
        s = jax.nn.sigmoid(p)
        act[:, cols] = (p * s).astype(BF16)
        dact[:, cols] = s * (1.0 + p * (1.0 - s))
        return carry

    lax.fori_loop(0, 4, project, 0)

    lane128 = lax.broadcasted_iota(jnp.int32, (ROWS, 128), 1)

    def pair_cols(base, p):
        return pl.ds(pl.multiple_of(base * D + p * 128, 128), 128)

    def attend(p, carry):
        v = act[:, pair_cols(1, p)]
        q = act[:, pair_cols(2, p)].astype(F32)
        k = act[:, pair_cols(3, p)]
        parts = []
        for h in range(2):
            inside = (lane128 // 64) == h
            qh = jnp.where(inside, q, 0.0).astype(BF16)
            scores = dot(qh, k, 1, 1)
            s = jax.nn.sigmoid(scores)
            allow = vis[...]
            wts = (scores * s * allow).astype(BF16)
            w8[2 * p + h] = wts
            d8[2 * p + h] = s * (1.0 + scores * (1.0 - s)) * allow
            parts.append(dot(wts, v, 1, 0))
        mixed[:, pl.ds(pl.multiple_of(p * 128, 128), 128)] = jnp.where(
            lane128 < 64, parts[0], parts[1]
        )
        return carry

    lax.fori_loop(0, HEADS // 2, attend, 0)

    m32 = mixed[...]
    m_center = jnp.mean(m32, axis=-1, keepdims=True)
    m_centred = m32 - m_center
    m_scale = lax.rsqrt(jnp.mean(m_centred * m_centred, axis=-1, keepdims=True) + EPS)
    m_normed = m_centred * m_scale
    mixed[...] = m_normed
    gated[...] = (m_normed * act[:, 0:D].astype(F32)).astype(BF16)
    layer = (dot(gated[...], weight(4), 1, 0) + xf[...]).astype(BF16)
    os_[...] = to_blocks(dot(ptr[...], layer, 1, 0))
    or_[z] = os_[z]
    exchange(2, os_, or_, 0, NZ - 1, True)

    exchange_wait(1, cr, True)
    cot = dot(ptr[...], rows_of(cr).astype(BF16), 0, 0)
    cot16 = cot.astype(BF16)
    xf[...] = cot
    p_c = [
        remote(pb.at[c, :, :, 1 - core], rc.at[c], rs_send.at[24 + c], rs_recv.at[24 + c], partner)
        for c in range(5)
    ]
    pb[4] = dot(gated[...], cot16, 0, 0).astype(BF16).reshape(4, 4, 2, 16, D)
    p_c[4].start()

    def weight_grad(c):
        part = dot(xn[...], gproj[:, c * D : (c + 1) * D], 0, 0)
        pb[c] = part.astype(BF16).reshape(4, 4, 2, 16, D)
        p_c[c].start()

    g_gated = dot(cot16, weight(4), 1, 1).astype(BF16).astype(F32)
    m_normed = mixed[...]
    g_normed = g_gated * act[:, 0:D].astype(F32)
    g_u = (g_gated * m_normed).astype(BF16).astype(F32)
    gproj[:, 0:D] = (g_u * dact[:, 0:D]).astype(BF16)
    weight_grad(0)
    g_mixed = m_scale * (
        g_normed
        - jnp.mean(g_normed, axis=-1, keepdims=True)
        - m_normed * jnp.mean(g_normed * m_normed, axis=-1, keepdims=True)
    )
    gated[...] = g_mixed.astype(BF16)

    def attend_back(p, carry):
        v = act[:, pair_cols(1, p)]
        q = act[:, pair_cols(2, p)]
        k = act[:, pair_cols(3, p)]
        gm = gated[:, pl.ds(pl.multiple_of(p * 128, 128), 128)]
        gv, gq, gk = [], [], []
        for h in range(2):
            inside = (lane128 // 64) == h
            gmh = jnp.where(inside, gm.astype(F32), 0.0).astype(BF16)
            g_w = dot(gmh, v, 1, 1).astype(BF16).astype(F32)
            g_s = (g_w * d8[2 * p + h]).astype(BF16)
            gv.append(dot(w8[2 * p + h], gm, 0, 0))
            gq.append(dot(g_s, k, 1, 0))
            gk.append(dot(g_s, q, 0, 0))
        for base, part in ((1, gv), (2, gq), (3, gk)):
            value = jnp.where(lane128 < 64, part[0], part[1]).astype(BF16).astype(F32)
            cols = pair_cols(base, p)
            gproj[:, cols] = (value * dact[:, cols]).astype(BF16)
        return carry

    lax.fori_loop(0, HEADS // 2, attend_back, 0)

    for c in range(1, 4):
        weight_grad(c)

    mixed[...] = dot(gproj[:, 0:D], weight(0), 1, 1)

    def input_grad(c, carry):
        cols = pl.ds(pl.multiple_of(c * D, D), D)
        mixed[...] = mixed[...] + dot(gproj[:, cols], weight(c), 1, 1)
        return carry

    lax.fori_loop(1, 4, input_grad, 0)
    def core_sum(c):
        def step(i, carry):
            y = i // 4
            x = i % 4
            total = (pb[c, y, x, core].astype(F32) + rc[c, y, x].astype(F32)).astype(BF16)
            sa[y, x // 2, x % 2, :, c * D : (c + 1) * D] = total[0:8]
            sb[x, y // 2, y % 2, :, c * D : (c + 1) * D] = total[8:16]
            return carry

        lax.fori_loop(0, 16, step, 0)

    for c in (4, 0, 1, 2, 3):
        p_c[c].wait_recv()
        core_sum(c)

    def ring_open(base, me, plus, minus, s, t, u):
        opp, nxt, prv = (me + 2) % 4, (me + 1) % 4, (me + 3) % 4
        plan = (
            (s.at[opp, 0], t.at[0], plus),
            (s.at[opp, 1], t.at[1], minus),
            (s.at[nxt, 1], u.at[0, 1], plus),
            (s.at[prv, 0], u.at[1, 0], minus),
            (s.at[nxt, 0], u.at[0, 0], plus),
            (s.at[prv, 1], u.at[1, 1], minus),
        )
        copies = [
            remote(src, dst, rs_send.at[base + i], rs_recv.at[base + i], dev)
            for i, (src, dst, dev) in enumerate(plan)
        ]
        for copy in copies[:4]:
            copy.start()
        return copies

    def ring_pass(copies, me, s, t):
        nxt, prv = (me + 1) % 4, (me + 3) % 4
        copies[0].wait_recv()
        s[nxt, 0] = (s[nxt, 0].astype(F32) + t[0].astype(F32)).astype(BF16)
        copies[4].start()
        copies[1].wait_recv()
        s[prv, 1] = (s[prv, 1].astype(F32) + t[1].astype(F32)).astype(BF16)
        copies[5].start()

    def ring_close(copies, me, s, u, h):
        return s[me, h].astype(F32) + u[0, h].astype(F32) + u[1, h].astype(F32)

    ca = ring_open(0, yy, yplus, yminus, sa, ta, ua)
    cb = ring_open(6, xx, xplus, xminus, sb, tb, ub)
    g_xn = mixed[...]
    zz = zf[...]
    g_x = inv[:, 0:1] * (
        g_xn
        - jnp.mean(g_xn, axis=-1, keepdims=True)
        - zz * jnp.mean(g_xn * zz, axis=-1, keepdims=True)
    ) + xf[...]
    gs[...] = to_blocks(dot(ptr[...], g_x.astype(BF16), 1, 0))
    gr[z] = gs[z]
    exchange(3, gs, gr, 0, 11, True)
    ring_pass(ca, yy, sa, ta)
    ring_pass(cb, xx, sb, tb)
    for copies in (ca, cb):
        for i in range(2, 6):
            copies[i].wait_recv()
    for h in range(2):
        total = ring_close(ca, yy, sa, ua, h).astype(BF16)
        for i in range(2):
            for q in range(2):
                sa2[2 * h + i, q] = total[i, :, q * HALF : (q + 1) * HALF]
    for h in range(2):
        total = ring_close(cb, xx, sb, ub, h).astype(BF16)
        for i in range(2):
            for q in range(2):
                sb2[2 * h + i, q] = total[i, :, q * HALF : (q + 1) * HALF]
    ca2 = ring_open(12, xx, xplus, xminus, sa2, ta2, ua2)
    cb2 = ring_open(18, yy, yplus, yminus, sb2, tb2, ub2)
    ring_pass(ca2, xx, sa2, ta2)
    ring_pass(cb2, yy, sb2, tb2)
    for copies in (ca2, cb2):
        for i in range(2, 6):
            copies[i].wait_recv()
    for which, (copies, me, s, u) in enumerate(((ca2, xx, sa2, ua2), (cb2, yy, sb2, ub2))):
        for h in range(2):
            total = ring_close(copies, me, s, u, h)
            for j in range(10):
                k = (h * 10 + j) * 2 + which
                z1[k // 5, k % 5] = total[:, 128 * j : 128 * j + 128].astype(BF16)

    shift = SEG // 2 * core
    seg = (z + shift) % NZ // SEG
    idx = (z + shift) % SEG

    def in_segment(d):
        i = (idx + d) % SEG
        return i, (g, (seg * SEG + i + NZ - shift) % NZ)

    def scatter_step(d, carry):
        i, dev = in_segment(d)
        remote(z1.at[i], r1.at[idx], ar_send.at[0], ar_recv.at[0], dev).start()
        return carry

    lax.fori_loop(1, SEG, scatter_step, 0)
    exchange(3, gs, gr, 11, 17, True)
    r1[idx] = z1[idx]
    seven = r1.at[pl.ds(0, SEG - 1)]
    remote(seven, seven, ar_send.at[0], ar_recv.at[0], partner).wait_recv()
    total = r1[0].astype(F32)
    for i in range(1, SEG):
        total = total + r1[i].astype(F32)
    z2[...] = total.astype(BF16)
    r2[seg] = z2[...]

    def segment_step(d, carry):
        remote(
            z2, r2.at[seg], ar_send.at[1], ar_recv.at[1], (g, (z + SEG * (d % 3 + 1)) % NZ)
        ).start()
        return carry

    lax.fori_loop(1, NSEG, segment_step, 0)
    exchange(3, gs, gr, 17, 25, True)

    three = r2.at[pl.ds(0, NSEG - 1)]
    remote(three, three, ar_send.at[1], ar_recv.at[1], partner).wait_recv()
    total = r2[0].astype(F32)
    for i in range(1, NSEG):
        total = total + r2[i].astype(F32)
    z3[...] = total.astype(BF16)
    r3[idx] = z3[...]

    def share_step(d, carry):
        i, dev = in_segment(d)
        remote(z3, r3.at[idx], ar_send.at[2], ar_recv.at[2], dev).start()
        return carry

    lax.fori_loop(1, SEG, share_step, 0)
    exchange(3, gs, gr, 25, NZ - 1, True)
    exchange_wait(2, or_, True)
    eight = r3.at[pl.ds(0, SEG - 1)]
    last = remote(eight, eight, ar_send.at[2], ar_recv.at[2], partner)
    last.wait_recv()
    exchange_wait(3, gr, True)

    for which, buf in enumerate((xs, cs, os_, gs)):
        exchange_wait(which, buf, False)
    for copy in (w_x0, w_x1, w_x2, w_x3, w_y0, w_y1, w_y2, w_y3, *w_c, *p_c):
        copy.wait_send()
    for copies in (ca, cb, ca2, cb2):
        for copy in copies:
            copy.wait_send()
    remote(seven, seven, ar_send.at[0], ar_recv.at[0], partner).wait_send()
    remote(three, three, ar_send.at[1], ar_recv.at[1], partner).wait_send()
    last.wait_send()


def finish(or_ref, gr_ref, sum_ref, sp_in, out_ref, grad_ref, gu_ref, go_ref):
    lane = lax.broadcasted_iota(jnp.int32, (1, ROWS), 1)
    index = lane % BLOCK
    for t in range(BLK):
        index = index + jnp.where(lane // BLOCK == t, sp_in[t] * BLOCK, 0)
    hot = lax.broadcasted_iota(jnp.int32, (ROWS, ROWS), 0) == index
    hot = hot.astype(F32).astype(BF16)
    for src, dst in ((or_ref, out_ref), (gr_ref, grad_ref)):
        rows = src[...].astype(F32).reshape(ROWS, D).astype(BF16)
        dst[...] = dot(hot, rows, 1, 0).astype(BF16)
    for k in range(40):
        j, r = k // 2, k % 2
        tile = sum_ref[k // 5, k % 5].astype(F32)
        if j < 16:
            gu_ref[8 * r : 8 * r + 8, 128 * j : 128 * j + 128] = tile
        else:
            go_ref[8 * r : 8 * r + 8, 128 * (j - 16) : 128 * (j - 15)] = tile


def on_device(inputs, cotangent, w_uvqk, w_out, send_perm, recv_perm, lengths, prefixes):
    vmem = pl.BlockSpec(memory_space=pltpu.VMEM)
    smem = pl.BlockSpec(memory_space=pltpu.SMEM)
    blocks = pltpu.VMEM((BLK, BLOCK, D), BF16)

    def buf(*shape, dtype=BF16):
        return pltpu.VMEM(shape, dtype)

    dma = pltpu.SemaphoreType.DMA
    send_order = send_perm[0, 0]
    back_out, back_grad, sums = pl.pallas_call(
        kernel,
        out_shape=(
            jax.ShapeDtypeStruct((BLK, BLOCK, D), BF16),
            jax.ShapeDtypeStruct((BLK, BLOCK, D), BF16),
            jax.ShapeDtypeStruct((SEG, 5, 8, 128), BF16),
        ),
        in_specs=[pl.BlockSpec(memory_space=pl.ANY)] * 4 + [smem] * 4,
        out_specs=(vmem,) * 3,
        scratch_shapes=[
            *([blocks] * 6),
            buf(4, 4, 2, 16, COLS),
            buf(5, 4, 4, 2, 16, D),
            buf(5, 4, 4, 16, D),
            buf(4, 2, 2, 8, COLS),
            buf(4, 2, 2, 8, COLS),
            buf(4, 2, 8, HALF),
            buf(4, 2, 8, HALF),
            buf(2, 2, 8, COLS),
            buf(2, 2, 8, COLS),
            buf(2, 8, HALF),
            buf(2, 8, HALF),
            buf(2, 2, 2, 8, COLS),
            buf(2, 2, 2, 8, COLS),
            buf(2, 2, 8, HALF),
            buf(2, 2, 8, HALF),
            buf(SEG, 5, 8, 128),
            buf(SEG, 5, 8, 128),
            buf(5, 8, 128),
            buf(NSEG, 5, 8, 128),
            buf(5, 8, 128),
            buf(ROWS, D),
            buf(ROWS, D),
            dma((4,)),
            buf(ROWS, ROWS),
            buf(ROWS, ROWS),
            buf(ROWS, ROWS, dtype=F32),
            buf(ROWS, D, dtype=F32),
            buf(ROWS, D, dtype=F32),
            buf(ROWS, 128, dtype=F32),
            buf(ROWS, D),
            buf(ROWS, 4 * D),
            buf(ROWS, 4 * D, dtype=F32),
            buf(ROWS, D, dtype=F32),
            buf(ROWS, D),
            buf(ROWS, 4 * D),
            buf(HEADS, ROWS, ROWS),
            buf(HEADS, ROWS, ROWS, dtype=F32),
            pltpu.SemaphoreType.REGULAR((2,)),
            dma((4,)),
            dma((4,)),
            dma((12,)),
            dma((12,)),
            dma((29,)),
            dma((29,)),
            dma((3,)),
            dma((3,)),
        ],
        compiler_params=pltpu.CompilerParams(
            collective_id=0, has_side_effects=True, vmem_limit_bytes=60 * 1024 * 1024
        ),
    )(
        inputs[0],
        cotangent[0],
        w_uvqk,
        w_out,
        send_order,
        recv_perm[0, 0],
        lengths[0, 0],
        prefixes[0, 0],
    )
    out, grad, gu, go = pl.pallas_call(
        finish,
        out_shape=(
            jax.ShapeDtypeStruct((ROWS, D), BF16),
            jax.ShapeDtypeStruct((ROWS, D), BF16),
            jax.ShapeDtypeStruct((16, 4 * D), F32),
            jax.ShapeDtypeStruct((16, D), F32),
        ),
        in_specs=[vmem] * 3 + [smem],
        out_specs=(vmem,) * 4,
    )(back_out, back_grad, sums, send_order)
    return (out[None], grad[None], gu, go)


def solution(mesh):
    rows = P("group", "shuf", None)
    return jax.shard_map(
        on_device,
        mesh=mesh,
        in_specs=(rows, rows, P("group", None), P("group", None), rows, rows, rows, rows),
        out_specs=(rows, rows, P("group", None), P("group", None)),
        check_vma=False,
    )
```
